32 devices in a mesh: tm: 8 (over y, x, core), space: 4 (over z).
Axes of the slice: x: 2, y: 2, z: 4, core: 2. Of those that a mesh axis runs over, the one named last changes fastest.
Arguments:
- panel: bfloat16 [8, 32, 2, 3, 4, 512], P('tm', None, None, None, 'space'), may hold values from -0.25 to 0.25
- gauge: bfloat16 [8, 4, 2, 3, 3, 4, 512], P('tm', None, None, None, None, 'space'), may hold values from -2.390625 to 2.390625
- momenta: int32 [8, 3], replicated, may hold values from -2 to 2
- op_momentum: int32 [8], replicated, may hold values from 0 to 7
- op_displacement: int32 [8], replicated, may hold values from 0 to 3
Outputs:
- elementals: float32 [8, 8, 2, 32, 32], P('space', 'tm')
The draws below stay inside these ranges and needn't reach their ends.
All inputs are finite; a program needn't handle non-finite values.
Results may differ from the reference program's by a relative error of at most 0.0038.
Values may be sent and summed in bfloat16 or wider, within the bound.
A program may use at most 64 MiB of HBM per device.

```python
import math
import jax
import jax.numpy as jnp
from jax import lax

VEC = 32
LY = 16
LZ = 32
NMOM = 8
NT = 8
LX = 4
NOP = 8


def place_ends(entries, own_key, low, largest):
    place = [jax.random.randint(jax.random.fold_in(own_key, axis), (), 0, length) for axis, length in enumerate(entries.shape)]
    longest = entries.shape.index(max(entries.shape))
    beside = place[:longest] + [(place[longest] + 1) % entries.shape[longest]] + place[longest + 1:]
    return entries.at[tuple(place)].set(low).at[tuple(beside)].set(largest)


def shard_levels(key, dims, pieces, smallest, high):
    level = 1.0
    for position, parts in pieces:
        steps = jax.random.uniform(jax.random.fold_in(jax.random.fold_in(key, 6), position), (parts,), jnp.float32, smallest / len(pieces), high / len(pieces))
        level = level * jnp.repeat(jnp.exp(steps), dims[position] // parts).reshape((-1,) + (1,) * (len(dims) - 1 - position))
    return level


def normal_values(rng, shape, scale, bound, pieces=(), held_as=jnp.bfloat16):
    result = jax.random.normal(rng, shape, jnp.float32) * scale
    if len(pieces) > 0:
        result = shard_levels(rng, shape, pieces, -0.22, 0.18) * result
    return jnp.clip(result, min=-bound, max=bound).astype(held_as)


def setup_inputs(seed: int = 0) -> dict:
    splits = jax.random.split(jax.random.key(seed), 6)
    return {
        "panel": normal_values(splits[0], (NT, VEC, 2, 3, LX, LY * LZ), (LY * LZ) ** -0.5, 0.25, ((0, 8), (4, 4))),
        "gauge": normal_values(splits[1], (NT, 4, 2, 3, 3, LX, LY * LZ), 0.4, 2.390625, ((0, 8), (5, 4))),
        "momenta": place_ends(jax.random.randint(splits[2], (NMOM, 3), -2, 3), jax.random.fold_in(splits[2], 1), -2, 2).astype(jnp.int32),
        "op_momentum": place_ends(jax.random.randint(splits[3], (NOP,), 0, NMOM), jax.random.fold_in(splits[3], 1), 0, NMOM - 1).astype(jnp.int32),
        "op_displacement": place_ends(jax.random.randint(splits[4], (NOP,), 0, 4), jax.random.fold_in(splits[4], 1), 0, 3).astype(jnp.int32),
    }


def link_times(gauge_link, source, adjoint):
    real_link = gauge_link[0]
    imag_link = gauge_link[1]
    if adjoint:
        real_link = jnp.swapaxes(real_link, 0, 1)
        imag_link = -jnp.swapaxes(imag_link, 0, 1)
    source_real = source[:, 0][:, None]
    source_imag = source[:, 1][:, None]
    out_real = jnp.sum(real_link[None] * source_real - imag_link[None] * source_imag, axis=2)
    out_imag = jnp.sum(real_link[None] * source_imag + imag_link[None] * source_real, axis=2)
    return jnp.stack([out_real, out_imag], axis=1)


def neighbour(source, direction, offset):
    if direction == 0:
        return jnp.roll(source, -offset, axis=-2)
    if direction == 1:
        return jnp.roll(source, -offset * LZ, axis=-1)
    field_shape = source.shape
    site_grid = source.reshape(field_shape[:-1] + (LY, LZ))
    return jnp.roll(site_grid, -offset, axis=-1).reshape(field_shape)


def phases(momentum_row, coord_x, coord_y, coord_z, extent_x):
    part_x = jnp.mod(momentum_row[0] * coord_x, extent_x).astype(jnp.float32) / extent_x
    part_y = jnp.mod(momentum_row[1] * coord_y, LY).astype(jnp.float32) / LY
    part_z = jnp.mod(momentum_row[2] * coord_z, LZ).astype(jnp.float32) / LZ
    angle_total = (2.0 * math.pi) * (part_x[:, None] + (part_y + part_z)[None, :])
    return jnp.cos(angle_total), jnp.sin(angle_total)


def rotate(source, cosine, sine_part):
    real_part = source[:, 0]
    imag_part = source[:, 1]
    return jnp.stack([cosine * real_part - sine_part * imag_part, cosine * imag_part + sine_part * real_part], axis=1).astype(jnp.bfloat16)


def contract(left_rows, right_rows):
    row_total = left_rows.shape[0]
    halves = left_rows.reshape(row_total, 2, -1)
    stacked = jnp.concatenate([halves.reshape(row_total, -1), jnp.concatenate([-halves[:, 1], halves[:, 0]], axis=1)], axis=0)
    flat_right = right_rows.reshape(right_rows.shape[0], -1)
    return jnp.dot(stacked, flat_right.T, preferred_element_type=jnp.float32)


def conj_transpose(matrix):
    vectors = matrix.shape[-1]
    real_part = matrix[..., :vectors, :]
    imag_part = matrix[..., vectors:, :]
    return jnp.concatenate([jnp.swapaxes(real_part, -1, -2), -jnp.swapaxes(imag_part, -1, -2)], axis=-2)


def reference(panel, gauge, momenta, op_momentum, op_displacement):
    slices = panel.shape[0]
    vectors = panel.shape[1]
    extent_x = panel.shape[4]
    site_count = panel.shape[5]
    moment_count = momenta.shape[0]
    coord_x = jnp.arange(extent_x, dtype=jnp.int32)
    site_index = jnp.arange(site_count, dtype=jnp.int32)
    coord_y = site_index // LZ
    coord_z = site_index % LZ

    def slice_terms(slice_index):
        current = panel[slice_index].astype(jnp.float32)
        upcoming = panel[(slice_index + 1) % slices].astype(jnp.float32)
        gauge_here = gauge[slice_index].astype(jnp.float32)
        hop_list = []
        for direction in range(3):
            forward = link_times(gauge_here[direction], neighbour(current, direction, 1), False)
            lower_link = neighbour(gauge_here[direction], direction, -1)
            backward = link_times(lower_link, neighbour(current, direction, -1), True)
            hop_list.append((forward - backward).astype(jnp.bfloat16))
        time_hop = link_times(gauge_here[3], upcoming, False).astype(jnp.bfloat16)
        right_all = jnp.concatenate(hop_list + [time_hop], axis=0)

        def per_moment(moment):
            cosine, sine_part = phases(momenta[moment], coord_x, coord_y, coord_z, extent_x)
            main_part = contract(rotate(current, cosine, sine_part), right_all)
            mirror_part = contract(rotate(current, cosine, -sine_part), time_hop)
            return main_part, mirror_part

        return lax.map(per_moment, jnp.arange(moment_count, dtype=jnp.int32))

    main_terms, mirror_terms = lax.map(slice_terms, jnp.arange(slices, dtype=jnp.int32))
    back_terms = conj_transpose(jnp.roll(mirror_terms, 1, axis=0))
    elemental_table = main_terms.reshape(slices, moment_count, 2 * vectors, 4, vectors).transpose(0, 1, 3, 2, 4)
    elemental_table = jnp.concatenate([elemental_table[:, :, :3], (elemental_table[:, :, 3] - back_terms)[:, :, None]], axis=2)
    picked = elemental_table[:, op_momentum, op_displacement]
    operators = op_momentum.shape[0]
    return picked.transpose(1, 0, 2, 3).reshape(operators, slices, 2, vectors, vectors)
```

```python
import functools
import math

import jax
import jax.numpy as jnp
from jax import lax
from jax.experimental import pallas as pl
from jax.experimental.pallas import tpu as pltpu
from jax.sharding import PartitionSpec as P

LY = 16
LZ = 32
F32 = jnp.float32
BF16 = jnp.bfloat16
COLOURS = 3
MESH = pl.DeviceIdType.MESH


def nt_dot(a, b):
    return lax.dot_general(a, b, (((1,), (1,)), ((), ())), preferred_element_type=F32)


def kernel(
    n_tm, n_space, v, g, mom, op_m, op_d, out,
    gf, gbf, cs, rot, back, hops, tmp, table, hx, ht, hb, gb, stage, got,
    send_sem, recv_sem,
):
    vectors, sites = v.shape[2], v.shape[3]
    moments = mom.shape[1]
    rows_here = out.shape[0]
    half = COLOURS * sites
    lanes = 128
    chunks = [slice(q * lanes, (q + 1) * lanes) for q in range(sites // lanes)]
    tm, space = lax.axis_index("tm"), lax.axis_index("space")
    tm_prev, tm_next = lax.rem(tm + n_tm - 1, n_tm), lax.rem(tm + 1, n_tm)
    space_prev = lax.rem(space + n_space - 1, n_space)

    barrier = pltpu.get_barrier_semaphore()
    for step in range(1, n_space):
        pl.semaphore_signal(
            barrier, inc=1, device_id=(tm, lax.rem(space + step, n_space)), device_id_type=MESH
        )
    for other in (tm_prev, tm_next):
        pl.semaphore_signal(barrier, inc=1, device_id=(other, space), device_id_type=MESH)
    pl.semaphore_wait(barrier, n_space + 1)

    def send(src, dst, index, device):
        copy = pltpu.make_async_remote_copy(
            src_ref=src, dst_ref=dst, send_sem=send_sem.at[index], recv_sem=recv_sem.at[index],
            device_id=device, device_id_type=MESH,
        )
        copy.start()
        return copy

    x_copies = [send(v.at[b], hx.at[b], b, (tm, space_prev)) for b in range(COLOURS)]
    t_copies = [
        send(v, ht, 3, (tm_prev, space)),
        send(v, hb, 4, (tm_next, space)),
        send(g.at[3], gb, 5, (tm_next, space)),
    ]

    gf[...] = g[...].astype(F32)

    def column(row):
        which = lax.broadcasted_iota(jnp.int32, (moments, sites), 0)
        value = jnp.zeros((moments, sites), jnp.int32)
        for m in range(moments):
            value = jnp.where(which == m, mom[row, m], value)
        return value

    site = lax.broadcasted_iota(jnp.int32, (moments, sites), 1)

    def part(momentum, coord, extent):
        turns = (momentum * coord).astype(F32) / extent
        return turns - jnp.floor(turns)

    px = column(0)
    part_yz = part(column(1), site // LZ, LY) + part(column(2), site % LZ, LZ)
    for shift in range(2):
        angle = (2.0 * math.pi) * (part(px, space + shift, n_space) + part_yz)
        for i, value in enumerate((jnp.cos(angle), jnp.sin(angle))):
            for m in range(moments):
                cs[2 * shift + i, m] = value[m : m + 1]

    def rotate(m, carry):
        rows = pl.ds(pl.multiple_of(m * vectors, vectors), vectors)
        for sl in chunks:
            c, s, cb, sb = (cs[i, m, :, sl] for i in range(4))
            for b in range(COLOURS):
                re = v[b, 0, :, sl].astype(F32)
                im = v[b, 1, :, sl].astype(F32)
                lo = slice(b * sites + sl.start, b * sites + sl.stop)
                hi = slice(half + lo.start, half + lo.stop)
                rot[rows, lo] = (c * re - s * im).astype(BF16)
                rot[rows, hi] = (c * im + s * re).astype(BF16)
                back[rows, lo] = (cb * re + sb * im).astype(BF16)
                back[rows, hi] = (cb * im - sb * re).astype(BF16)
        return carry

    lax.fori_loop(0, moments, rotate, 0)

    def link_row(links, mu, part_index, a, b, sl):
        row = part_index * COLOURS * COLOURS + a * COLOURS + b
        if mu is None:
            return links[row : row + 1, sl]
        return links[mu, row : row + 1, sl]

    def times(links, mu, source, sl, adjoint):
        src = [(source(b, 0, sl), source(b, 1, sl)) for b in range(COLOURS)]
        result = []
        for a in range(COLOURS):
            re = im = None
            for b in range(COLOURS):
                row, col = (b, a) if adjoint else (a, b)
                ur = link_row(links, mu, 0, row, col, sl)
                ui = link_row(links, mu, 1, row, col, sl)
                sr, si = src[b]
                if adjoint:
                    r, i = ur * sr + ui * si, ur * si - ui * sr
                else:
                    r, i = ur * sr - ui * si, ur * si + ui * sr
                re, im = (r, i) if re is None else (re + r, im + i)
            result.append((re, im))
        return result

    def put(d, a, sl, re, im):
        lo = slice(a * sites + sl.start, a * sites + sl.stop)
        hi = slice(half + lo.start, half + lo.stop)
        re, im = re.astype(BF16), im.astype(BF16)
        hops[d, :vectors, lo] = re
        hops[d, :vectors, hi] = im
        hops[d, vectors:, lo] = im
        hops[d, vectors:, hi] = -re

    in_z = lax.broadcasted_iota(jnp.int32, (vectors, sites), 1) % LZ

    def moved(value, direction, offset):
        if direction == 1:
            return pltpu.roll(value, (-offset * LZ) % sites, 1)
        near = pltpu.roll(value, -offset % sites, 1)
        wrap = pltpu.roll(value, (offset * (LZ - 1)) % sites, 1)
        edge = LZ - 1 if offset == 1 else 0
        return jnp.where(in_z == edge, wrap, near)

    def here(b, c, sl):
        return v[b, c, :, sl].astype(F32)

    whole = slice(0, sites)
    for d in (1, 2):
        for sl in chunks:
            for a, pair in enumerate(times(gf, d, here, sl, True)):
                for c in range(2):
                    tmp[1, a, c, :, sl] = pair[c]
        for a in range(COLOURS):
            for c in range(2):
                tmp[0, a, c] = moved(v[a, c].astype(F32), d, 1)
                tmp[1, a, c] = moved(tmp[1, a, c], d, -1)
        for sl in chunks:
            ahead = times(gf, d, lambda b, c, sl: tmp[0, b, c, :, sl], sl, False)
            for a, (re, im) in enumerate(ahead):
                put(d, a, sl, re - tmp[1, a, 0, :, sl], im - tmp[1, a, 1, :, sl])

    def fill(d):
        table[d] = nt_dot(rot[...], hops[d]).reshape(moments, vectors, 2 * vectors)

    fill(1)
    fill(2)

    for copy in t_copies:
        copy.wait()
    gbf[...] = gb[...].astype(F32)
    for sl in chunks:
        behind = times(gbf, None, lambda b, c, sl: hb[b, c, :, sl].astype(F32), sl, True)
        ahead = times(gf, 3, lambda b, c, sl: ht[b, c, :, sl].astype(F32), sl, False)
        for a in range(COLOURS):
            put(3, a, sl, ahead[a][0] - behind[a][0], ahead[a][1] - behind[a][1])
    fill(3)

    for copy in x_copies:
        copy.wait()
    for sl in chunks:
        ahead = times(gf, 0, lambda b, c, sl: hx[b, c, :, sl].astype(F32), sl, False)
        for a, (re, im) in enumerate(ahead):
            put(0, a, sl, re, im)
    mirror = nt_dot(hops[0], back[...])
    direct = nt_dot(rot[...], hops[0])
    for m in range(moments):
        cols = slice(m * vectors, (m + 1) * vectors)
        flipped = jnp.concatenate([mirror[:vectors, cols], -mirror[vectors:, cols]], axis=1)
        table[0, m] = direct[cols] - flipped

    sums = []
    for step in range(n_space):
        owner = lax.rem(space + step, n_space)
        for r in range(rows_here):
            k = owner * rows_here + r
            stage[step, :, r * 2 * vectors : (r + 1) * 2 * vectors] = table[op_d[k], op_m[k]]
        if step > 0:
            sums.append(send(stage.at[step], got.at[step - 1], 5 + step, (tm, owner)))
    total = stage[0]
    for step, copy in enumerate(sums):
        copy.wait()
        total = total + got[step]
    for r in range(rows_here):
        for c in range(2):
            start = (2 * r + c) * vectors
            out[r, c] = total[:, start : start + vectors]


def solution(mesh):
    n_tm, n_space = mesh.shape["tm"], mesh.shape["space"]

    def shards(panel, gauge, momenta, op_momentum, op_displacement):
        vectors, sites = panel.shape[1], panel.shape[5]
        moments = momenta.shape[0]
        rows_here = op_momentum.shape[0] // n_space
        links = 2 * COLOURS * COLOURS
        v = panel[0, :, :, :, 0].transpose(2, 1, 0, 3)
        g = gauge[0, :, :, :, :, 0].reshape(4, links, sites)
        wide = 2 * COLOURS * sites
        vmem = pl.BlockSpec(memory_space=pltpu.VMEM)
        smem = pl.BlockSpec(memory_space=pltpu.SMEM)
        out = pl.pallas_call(
            functools.partial(kernel, n_tm, n_space),
            out_shape=jax.ShapeDtypeStruct((rows_here, 2, vectors, vectors), F32),
            in_specs=[vmem, vmem, smem, smem, smem],
            out_specs=vmem,
            scratch_shapes=[
                pltpu.VMEM((4, links, sites), F32),
                pltpu.VMEM((links, sites), F32),
                pltpu.VMEM((4, moments, 1, sites), F32),
                pltpu.VMEM((moments * vectors, wide), BF16),
                pltpu.VMEM((moments * vectors, wide), BF16),
                pltpu.VMEM((4, 2 * vectors, wide), BF16),
                pltpu.VMEM((2, COLOURS, 2, vectors, sites), F32),
                pltpu.VMEM((4, moments, vectors, 2 * vectors), F32),
                pltpu.VMEM((COLOURS, 2, vectors, sites), BF16),
                pltpu.VMEM((COLOURS, 2, vectors, sites), BF16),
                pltpu.VMEM((COLOURS, 2, vectors, sites), BF16),
                pltpu.VMEM((links, sites), BF16),
                pltpu.VMEM((n_space, vectors, rows_here * 2 * vectors), F32),
                pltpu.VMEM((n_space - 1, vectors, rows_here * 2 * vectors), F32),
                pltpu.SemaphoreType.DMA((5 + n_space,)),
                pltpu.SemaphoreType.DMA((5 + n_space,)),
            ],
            compiler_params=pltpu.CompilerParams(collective_id=0, has_side_effects=True),
        )(v, g, momenta.T, op_momentum, op_displacement)
        return out[:, None]

    placed = (
        P("tm", None, None, None, "space", None),
        P("tm", None, None, None, None, "space", None),
        P(),
        P(),
        P(),
    )
    return jax.shard_map(
        shards,
        mesh=mesh,
        in_specs=placed,
        out_specs=P("space", "tm", None, None, None),
        check_vma=False,
    )
```

```python
import functools
import math

import jax
import jax.numpy as jnp
from jax import lax
from jax.experimental import pallas as pl
from jax.experimental.pallas import tpu as pltpu
from jax.sharding import PartitionSpec as P

LY = 16
LZ = 32
F32 = jnp.float32
BF16 = jnp.bfloat16
COLOURS = 3
MESH = pl.DeviceIdType.MESH


def nt_dot(a, b):
    return lax.dot_general(a, b, (((1,), (1,)), ((), ())), preferred_element_type=F32)


def kernel(
    n_tm, n_space, panel, gauge, mom, op_m, op_d, out,
    raw, links, vf, gf, gbf, cs, rot, back, hops, tmp, table, hx, ht, hb, gb, stage, got,
    local_sem, send_sem, recv_sem,
):
    vectors, sites = raw.shape[0], raw.shape[3]
    moments = mom.shape[1]
    rows_here = out.shape[0]
    half = COLOURS * sites
    lanes = 128
    chunks = [slice(q * lanes, (q + 1) * lanes) for q in range(sites // lanes)]
    tm, space = lax.axis_index("tm"), lax.axis_index("space")
    tm_prev, tm_next = lax.rem(tm + n_tm - 1, n_tm), lax.rem(tm + 1, n_tm)
    space_prev = lax.rem(space + n_space - 1, n_space)

    barrier = pltpu.get_barrier_semaphore()
    for step in range(1, n_space):
        pl.semaphore_signal(
            barrier, inc=1, device_id=(tm, lax.rem(space + step, n_space)), device_id_type=MESH
        )
    for other in (tm_prev, tm_next):
        pl.semaphore_signal(barrier, inc=1, device_id=(other, space), device_id_type=MESH)
    loads = [
        pltpu.make_async_copy(panel, raw, local_sem.at[0]),
        pltpu.make_async_copy(gauge, links, local_sem.at[1]),
    ]
    for copy in loads:
        copy.start()
    pl.semaphore_wait(barrier, n_space + 1)

    def send(src, dst, index, device):
        copy = pltpu.make_async_remote_copy(
            src_ref=src, dst_ref=dst, send_sem=send_sem.at[index], recv_sem=recv_sem.at[index],
            device_id=device, device_id_type=MESH,
        )
        copy.start()
        return copy

    x_copies, t_copies = [], []
    for b in range(COLOURS):
        x_copies.append(send(panel.at[:, b], hx.at[:, b], b, (tm, space_prev)))
        t_copies.append([
            send(panel.at[:, b], ht.at[:, b], COLOURS + b, (tm_prev, space)),
            send(panel.at[:, b], hb.at[:, b], 2 * COLOURS + b, (tm_next, space)),
        ])
        if b == 0:
            t_copies[0].append(send(gauge.at[3], gb, 3 * COLOURS, (tm_next, space)))

    for copy in loads:
        copy.wait()
    gf[...] = links[...].astype(F32)
    for b in range(COLOURS):
        for c in range(2):
            vf[b, c] = raw[:, b, c].astype(F32)

    def column(row):
        which = lax.broadcasted_iota(jnp.int32, (moments, sites), 0)
        value = jnp.zeros((moments, sites), jnp.int32)
        for m in range(moments):
            value = jnp.where(which == m, mom[row, m], value)
        return value

    site = lax.broadcasted_iota(jnp.int32, (moments, sites), 1)

    def part(momentum, coord, extent):
        turns = (momentum * coord).astype(F32) / extent
        return turns - jnp.floor(turns)

    px = column(0)
    part_yz = part(column(1), site // LZ, LY) + part(column(2), site % LZ, LZ)
    for shift in range(2):
        angle = (2.0 * math.pi) * (part(px, space + shift, n_space) + part_yz)
        for i, value in enumerate((jnp.cos(angle), jnp.sin(angle))):
            for m in range(moments):
                cs[2 * shift + i, m] = value[m : m + 1]

    def rotate(m, carry):
        rows = pl.ds(pl.multiple_of(m * vectors, vectors), vectors)
        for sl in chunks:
            c, s, cb, sb = (cs[i, m, :, sl] for i in range(4))
            for b in range(COLOURS):
                re, im = vf[b, 0, :, sl], vf[b, 1, :, sl]
                lo = slice(b * sites + sl.start, b * sites + sl.stop)
                hi = slice(half + lo.start, half + lo.stop)
                rot[rows, lo] = (c * re - s * im).astype(BF16)
                rot[rows, hi] = (c * im + s * re).astype(BF16)
                back[rows, lo] = (cb * re + sb * im).astype(BF16)
                back[rows, hi] = (cb * im - sb * re).astype(BF16)
        return carry

    lax.fori_loop(0, moments, rotate, 0)

    def link_term(field, sr, si, a, b, sl, adjoint):
        at = (b, a) if adjoint else (a, b)
        ur, ui = (field[(*at, slice(c, c + 1), sl)] for c in range(2))
        if adjoint:
            return ur * sr + ui * si, ur * si - ui * sr
        return ur * sr - ui * si, ur * si + ui * sr

    def times(field, source, sl, adjoint):
        src = [(source[b, 0, :, sl], source[b, 1, :, sl]) for b in range(COLOURS)]
        result = []
        for a in range(COLOURS):
            terms = [link_term(field, *src[b], a, b, sl, adjoint) for b in range(COLOURS)]
            result.append(tuple(sum(t[c] for t in terms[1:]) + terms[0][c] for c in range(2)))
        return result

    def put(d, a, sl, re, im):
        lo = slice(a * sites + sl.start, a * sites + sl.stop)
        hi = slice(half + lo.start, half + lo.stop)
        re, im = re.astype(BF16), im.astype(BF16)
        hops[d, :vectors, lo] = re
        hops[d, :vectors, hi] = im
        hops[d, vectors:, lo] = im
        hops[d, vectors:, hi] = -re

    in_z = lax.broadcasted_iota(jnp.int32, (vectors, sites), 1) % LZ

    def moved(value, direction, offset):
        if direction == 1:
            return pltpu.roll(value, (-offset * LZ) % sites, 1)
        near = pltpu.roll(value, -offset % sites, 1)
        wrap = pltpu.roll(value, (offset * (LZ - 1)) % sites, 1)
        edge = LZ - 1 if offset == 1 else 0
        return jnp.where(in_z == edge, wrap, near)

    for d in (1, 2):
        for sl in chunks:
            for a, pair in enumerate(times(gf.at[d], vf, sl, True)):
                for c in range(2):
                    tmp[1, a, c, :, sl] = pair[c]
        for a in range(COLOURS):
            for c in range(2):
                tmp[0, a, c] = moved(vf[a, c], d, 1)
                tmp[1, a, c] = moved(tmp[1, a, c], d, -1)
        for sl in chunks:
            for a, (re, im) in enumerate(times(gf.at[d], tmp.at[0], sl, False)):
                put(d, a, sl, re - tmp[1, a, 0, :, sl], im - tmp[1, a, 1, :, sl])

    def fill(d):
        table[d] = nt_dot(rot[...], hops[d]).reshape(moments, vectors, 2 * vectors)

    fill(1)
    fill(2)

    def arrive(d, b):
        for sl in chunks:
            total = [[None] * 2 for _ in range(COLOURS)]
            parts = [(gf.at[0], hx, False)] if d == 0 else [(gf.at[3], ht, False), (gbf, hb, True)]
            for field, held, adjoint in parts:
                sr, si = (held[:, b, c, sl].astype(F32) for c in range(2))
                for a in range(COLOURS):
                    pair = link_term(field, sr, si, a, b, sl, adjoint)
                    for c in range(2):
                        value = pair[c]
                        if total[a][c] is not None:
                            value = total[a][c] - value
                        total[a][c] = value
            slot = 0 if d == 0 else 1
            for a in range(COLOURS):
                if b > 0:
                    total[a] = [tmp[slot, a, c, :, sl] + total[a][c] for c in range(2)]
                if b < COLOURS - 1:
                    for c in range(2):
                        tmp[slot, a, c, :, sl] = total[a][c]
                else:
                    put(d, a, sl, *total[a])

    for b in range(COLOURS):
        x_copies[b].wait()
        arrive(0, b)
        if b == COLOURS - 1:
            mirror = nt_dot(hops[0], back[...])
            direct = nt_dot(rot[...], hops[0])
            for m in range(moments):
                cols = slice(m * vectors, (m + 1) * vectors)
                flipped = jnp.concatenate([mirror[:vectors, cols], -mirror[vectors:, cols]], axis=1)
                table[0, m] = direct[cols] - flipped
        for copy in t_copies[b]:
            copy.wait()
        if b == 0:
            gbf[...] = gb[...].astype(F32)
        arrive(3, b)
    fill(3)

    sums = []
    for step in range(n_space):
        owner = lax.rem(space + step, n_space)
        for r in range(rows_here):
            k = owner * rows_here + r
            stage[step, :, r * 2 * vectors : (r + 1) * 2 * vectors] = table[op_d[k], op_m[k]]
        if step > 0:
            sums.append(send(stage.at[step], got.at[step - 1], 3 * COLOURS + step, (tm, owner)))
    total = stage[0]
    for step, copy in enumerate(sums):
        copy.wait()
        total = total + got[step]
    for r in range(rows_here):
        for c in range(2):
            start = (2 * r + c) * vectors
            out[r, c] = total[:, start : start + vectors]


def solution(mesh):
    n_tm, n_space = mesh.shape["tm"], mesh.shape["space"]

    def shards(panel, gauge, momenta, op_momentum, op_displacement):
        vectors, sites = panel.shape[1], panel.shape[5]
        moments = momenta.shape[0]
        rows_here = op_momentum.shape[0] // n_space
        v = panel[0, :, :, :, 0].transpose(0, 2, 1, 3)
        g = gauge[0, :, :, :, :, 0].transpose(0, 2, 3, 1, 4)
        wide = 2 * COLOURS * sites
        vmem = pl.BlockSpec(memory_space=pltpu.VMEM)
        smem = pl.BlockSpec(memory_space=pltpu.SMEM)
        hbm = pl.BlockSpec(memory_space=pl.ANY)
        sends = 3 * COLOURS + n_space
        out = pl.pallas_call(
            functools.partial(kernel, n_tm, n_space),
            out_shape=jax.ShapeDtypeStruct((rows_here, 2, vectors, vectors), F32),
            in_specs=[hbm, hbm, smem, smem, smem],
            out_specs=vmem,
            scratch_shapes=[
                pltpu.VMEM(v.shape, BF16),
                pltpu.VMEM(g.shape, BF16),
                pltpu.VMEM((COLOURS, 2, vectors, sites), F32),
                pltpu.VMEM(g.shape, F32),
                pltpu.VMEM(g.shape[1:], F32),
                pltpu.VMEM((4, moments, 1, sites), F32),
                pltpu.VMEM((moments * vectors, wide), BF16),
                pltpu.VMEM((moments * vectors, wide), BF16),
                pltpu.VMEM((4, 2 * vectors, wide), BF16),
                pltpu.VMEM((2, COLOURS, 2, vectors, sites), F32),
                pltpu.VMEM((4, moments, vectors, 2 * vectors), F32),
                pltpu.VMEM(v.shape, BF16),
                pltpu.VMEM(v.shape, BF16),
                pltpu.VMEM(v.shape, BF16),
                pltpu.VMEM(g.shape[1:], BF16),
                pltpu.VMEM((n_space, vectors, rows_here * 2 * vectors), F32),
                pltpu.VMEM((n_space - 1, vectors, rows_here * 2 * vectors), F32),
                pltpu.SemaphoreType.DMA((2,)),
                pltpu.SemaphoreType.DMA((sends,)),
                pltpu.SemaphoreType.DMA((sends,)),
            ],
            compiler_params=pltpu.CompilerParams(collective_id=0, has_side_effects=True),
        )(v, g, momenta.T, op_momentum, op_displacement)
        return out[:, None]

    placed = (
        P("tm", None, None, None, "space", None),
        P("tm", None, None, None, None, "space", None),
        P(),
        P(),
        P(),
    )
    return jax.shard_map(
        shards,
        mesh=mesh,
        in_specs=placed,
        out_specs=P("space", "tm", None, None, None),
        check_vma=False,
    )
```

```python
import functools
import math

import jax
import jax.numpy as jnp
from jax import lax
from jax.experimental import pallas as pl
from jax.experimental.pallas import tpu as pltpu
from jax.sharding import PartitionSpec as P

LY = 16
LZ = 32
F32 = jnp.float32
BF16 = jnp.bfloat16
COLOURS = 3
MESH = pl.DeviceIdType.MESH


def nt_dot(a, b):
    return lax.dot_general(a, b, (((1,), (1,)), ((), ())), preferred_element_type=F32)


def kernel(
    n_tm, n_space, panel, gauge, mom, op_m, op_d, out,
    raw, links, vf, gf, gbf, cs, rot, back, hops, tmp, table, hx, ht, hb, gb, mine, stage, got,
    local_sem, send_sem, recv_sem,
):
    vectors, sites = raw.shape[0], raw.shape[3]
    moments = mom.shape[1]
    rows_here = out.shape[1] // (2 * vectors)
    half = COLOURS * sites
    lanes = 128
    chunks = [slice(q * lanes, (q + 1) * lanes) for q in range(sites // lanes)]
    tm, space = lax.axis_index("tm"), lax.axis_index("space")
    tm_prev, tm_next = lax.rem(tm + n_tm - 1, n_tm), lax.rem(tm + 1, n_tm)
    space_prev = lax.rem(space + n_space - 1, n_space)

    barrier = pltpu.get_barrier_semaphore()
    for step in range(1, n_space):
        pl.semaphore_signal(
            barrier, inc=1, device_id=(tm, lax.rem(space + step, n_space)), device_id_type=MESH
        )
    for other in (tm_prev, tm_next):
        pl.semaphore_signal(barrier, inc=1, device_id=(other, space), device_id_type=MESH)
    loads = [
        pltpu.make_async_copy(panel, raw, local_sem.at[0]),
        pltpu.make_async_copy(gauge, links, local_sem.at[1]),
    ]
    for copy in loads:
        copy.start()

    def send(src, dst, index, device):
        copy = pltpu.make_async_remote_copy(
            src_ref=src, dst_ref=dst, send_sem=send_sem.at[index], recv_sem=recv_sem.at[index],
            device_id=device, device_id_type=MESH,
        )
        copy.start()
        return copy

    for copy in loads:
        copy.wait()
    gf[...] = links[...].astype(F32)
    for b in range(COLOURS):
        for c in range(2):
            vf[b, c] = raw[:, b, c].astype(F32)

    def column(row):
        which = lax.broadcasted_iota(jnp.int32, (moments, sites), 0)
        value = jnp.zeros((moments, sites), jnp.int32)
        for m in range(moments):
            value = jnp.where(which == m, mom[row, m], value)
        return value

    site = lax.broadcasted_iota(jnp.int32, (moments, sites), 1)

    def part(momentum, coord, extent):
        turns = (momentum * coord).astype(F32) / extent
        return turns - jnp.floor(turns)

    px = column(0)
    part_yz = part(column(1), site // LZ, LY) + part(column(2), site % LZ, LZ)
    for shift in range(2):
        angle = (2.0 * math.pi) * (part(px, space + shift, n_space) + part_yz)
        for i, value in enumerate((jnp.cos(angle), jnp.sin(angle))):
            for m in range(moments):
                cs[2 * shift + i, m] = value[m : m + 1]

    pl.semaphore_wait(barrier, n_space + 1)
    x_copies, t_copies = [], []
    for b in range(COLOURS):
        x_copies.append(send(panel.at[:, b], hx.at[:, b], b, (tm, space_prev)))
        t_copies.append([
            send(panel.at[:, b], ht.at[:, b], COLOURS + b, (tm_prev, space)),
            send(panel.at[:, b], hb.at[:, b], 2 * COLOURS + b, (tm_next, space)),
        ])
        if b == 0:
            t_copies[0].append(send(gauge.at[3], gb, 3 * COLOURS, (tm_next, space)))

    def rotate(m, carry):
        rows = pl.ds(pl.multiple_of(m * vectors, vectors), vectors)
        for sl in chunks:
            c, s, cb, sb = (cs[i, m, :, sl] for i in range(4))
            for b in range(COLOURS):
                re, im = vf[b, 0, :, sl], vf[b, 1, :, sl]
                lo = slice(b * sites + sl.start, b * sites + sl.stop)
                hi = slice(half + lo.start, half + lo.stop)
                rot[rows, lo] = (c * re - s * im).astype(BF16)
                rot[rows, hi] = (c * im + s * re).astype(BF16)
                back[rows, lo] = (cb * re + sb * im).astype(BF16)
                back[rows, hi] = (cb * im - sb * re).astype(BF16)
        return carry

    lax.fori_loop(0, moments, rotate, 0)

    def link_term(field, sr, si, a, b, sl, adjoint):
        at = (b, a) if adjoint else (a, b)
        ur, ui = (field[(*at, slice(c, c + 1), sl)] for c in range(2))
        if adjoint:
            return ur * sr + ui * si, ur * si - ui * sr
        return ur * sr - ui * si, ur * si + ui * sr

    def times(field, source, sl, adjoint):
        src = [(source[b, 0, :, sl], source[b, 1, :, sl]) for b in range(COLOURS)]
        result = []
        for a in range(COLOURS):
            terms = [link_term(field, *src[b], a, b, sl, adjoint) for b in range(COLOURS)]
            result.append(tuple(sum(t[c] for t in terms[1:]) + terms[0][c] for c in range(2)))
        return result

    def put(d, a, sl, re, im):
        lo = slice(a * sites + sl.start, a * sites + sl.stop)
        hi = slice(half + lo.start, half + lo.stop)
        re, im = re.astype(BF16), im.astype(BF16)
        hops[d, :vectors, lo] = re
        hops[d, :vectors, hi] = im
        hops[d, vectors:, lo] = im
        hops[d, vectors:, hi] = -re

    in_z = lax.broadcasted_iota(jnp.int32, (vectors, sites), 1) % LZ

    def moved(value, direction, offset):
        if direction == 1:
            return pltpu.roll(value, (-offset * LZ) % sites, 1)
        near = pltpu.roll(value, -offset % sites, 1)
        wrap = pltpu.roll(value, (offset * (LZ - 1)) % sites, 1)
        edge = LZ - 1 if offset == 1 else 0
        return jnp.where(in_z == edge, wrap, near)

    for d in (1, 2):
        for sl in chunks:
            for a, pair in enumerate(times(gf.at[d], vf, sl, True)):
                for c in range(2):
                    tmp[1, a, c, :, sl] = pair[c]
        for a in range(COLOURS):
            for c in range(2):
                tmp[0, a, c] = moved(vf[a, c], d, 1)
                tmp[1, a, c] = moved(tmp[1, a, c], d, -1)
        for sl in chunks:
            for a, (re, im) in enumerate(times(gf.at[d], tmp.at[0], sl, False)):
                put(d, a, sl, re - tmp[1, a, 0, :, sl], im - tmp[1, a, 1, :, sl])

    def fill(d):
        table[d] = nt_dot(rot[...], hops[d]).reshape(moments, vectors, 2 * vectors)

    fill(1)
    fill(2)

    def arrive(d, b):
        for sl in chunks:
            total = [[None] * 2 for _ in range(COLOURS)]
            parts = [(gf.at[0], hx, False)] if d == 0 else [(gf.at[3], ht, False), (gbf, hb, True)]
            for field, held, adjoint in parts:
                sr, si = (held[:, b, c, sl].astype(F32) for c in range(2))
                for a in range(COLOURS):
                    pair = link_term(field, sr, si, a, b, sl, adjoint)
                    for c in range(2):
                        value = pair[c]
                        if total[a][c] is not None:
                            value = total[a][c] - value
                        total[a][c] = value
            slot = 0 if d == 0 else 1
            for a in range(COLOURS):
                if b > 0:
                    total[a] = [tmp[slot, a, c, :, sl] + total[a][c] for c in range(2)]
                if b < COLOURS - 1:
                    for c in range(2):
                        tmp[slot, a, c, :, sl] = total[a][c]
                else:
                    put(d, a, sl, *total[a])

    for b in range(COLOURS):
        x_copies[b].wait()
        arrive(0, b)
        if b == COLOURS - 1:
            mirror = nt_dot(hops[0], back[...])
            direct = nt_dot(rot[...], hops[0])
            for m in range(moments):
                cols = slice(m * vectors, (m + 1) * vectors)
                flipped = jnp.concatenate([mirror[:vectors, cols], -mirror[vectors:, cols]], axis=1)
                table[0, m] = direct[cols] - flipped
        for copy in t_copies[b]:
            copy.wait()
        if b == 0:
            gbf[...] = gb[...].astype(F32)
        arrive(3, b)
    fill(3)

    sums = []
    for step in range(n_space):
        owner = lax.rem(space + step, n_space)
        for r in range(rows_here):
            k = owner * rows_here + r
            picked = table[op_d[k], op_m[k]]
            cols = slice(r * 2 * vectors, (r + 1) * 2 * vectors)
            if step == 0:
                mine[:, cols] = picked
            else:
                stage[step - 1, :, cols] = picked.astype(BF16)
        if step > 0:
            sums.append(send(stage.at[step - 1], got.at[step - 1], 3 * COLOURS + step, (tm, owner)))
    total = mine[...]
    for step, copy in enumerate(sums):
        copy.wait()
        total = total + got[step].astype(F32)
    out[...] = total


def solution(mesh):
    n_tm, n_space = mesh.shape["tm"], mesh.shape["space"]

    def shards(panel, gauge, momenta, op_momentum, op_displacement):
        vectors, sites = panel.shape[1], panel.shape[5]
        moments = momenta.shape[0]
        rows_here = op_momentum.shape[0] // n_space
        v = panel[0, :, :, :, 0].transpose(0, 2, 1, 3)
        g = gauge[0, :, :, :, :, 0].transpose(0, 2, 3, 1, 4)
        wide = 2 * COLOURS * sites
        vmem = pl.BlockSpec(memory_space=pltpu.VMEM)
        smem = pl.BlockSpec(memory_space=pltpu.SMEM)
        hbm = pl.BlockSpec(memory_space=pl.ANY)
        sends = 3 * COLOURS + n_space
        out = pl.pallas_call(
            functools.partial(kernel, n_tm, n_space),
            out_shape=jax.ShapeDtypeStruct((vectors, rows_here * 2 * vectors), F32),
            in_specs=[hbm, hbm, smem, smem, smem],
            out_specs=vmem,
            scratch_shapes=[
                pltpu.VMEM(v.shape, BF16),
                pltpu.VMEM(g.shape, BF16),
                pltpu.VMEM((COLOURS, 2, vectors, sites), F32),
                pltpu.VMEM(g.shape, F32),
                pltpu.VMEM(g.shape[1:], F32),
                pltpu.VMEM((4, moments, 1, sites), F32),
                pltpu.VMEM((moments * vectors, wide), BF16),
                pltpu.VMEM((moments * vectors, wide), BF16),
                pltpu.VMEM((4, 2 * vectors, wide), BF16),
                pltpu.VMEM((2, COLOURS, 2, vectors, sites), F32),
                pltpu.VMEM((4, moments, vectors, 2 * vectors), F32),
                pltpu.VMEM(v.shape, BF16),
                pltpu.VMEM(v.shape, BF16),
                pltpu.VMEM(v.shape, BF16),
                pltpu.VMEM(g.shape[1:], BF16),
                pltpu.VMEM((vectors, rows_here * 2 * vectors), F32),
                pltpu.VMEM((n_space - 1, vectors, rows_here * 2 * vectors), BF16),
                pltpu.VMEM((n_space - 1, vectors, rows_here * 2 * vectors), BF16),
                pltpu.SemaphoreType.DMA((2,)),
                pltpu.SemaphoreType.DMA((sends,)),
                pltpu.SemaphoreType.DMA((sends,)),
            ],
            compiler_params=pltpu.CompilerParams(collective_id=0, has_side_effects=True),
        )(v, g, momenta.T, op_momentum, op_displacement)
        return out.reshape(vectors, rows_here, 2, vectors).transpose(1, 2, 0, 3)[:, None]

    placed = (
        P("tm", None, None, None, "space", None),
        P("tm", None, None, None, None, "space", None),
        P(),
        P(),
        P(),
    )
    return jax.shard_map(
        shards,
        mesh=mesh,
        in_specs=placed,
        out_specs=P("space", "tm", None, None, None),
        check_vma=False,
    )
```
